512 devices in a mesh: section: 16 (over z_lo, x), peer: 32 (over z_hi, y, core).
Axes of the slice: x: 4, y: 8, z: 8 (z_hi: 2, z_lo: 4; z = z_hi * 4 + z_lo), core: 2. Of those that a mesh axis runs over, the one named last changes fastest.
Arguments:
- inbox: bfloat16 [16, 32, 128, 5120], P('section', 'peer'), may hold values from -6 to 6
- routes: int32 [16, 32, 32], replicated, may hold values from 0 to 1, as said below
- adapter_in: bfloat16 [16, 2, 16, 5120], P('section'), may hold values from -0.078125 to 0.078125
- adapter_out: bfloat16 [16, 2, 16, 5120], P('section'), may hold values from -1.5 to 1.5
- returned: bfloat16 [16, 32, 160, 5120], P('section', 'peer'), may hold values from -6 to 6
Outputs:
- handed: bfloat16 [16, 32, 160, 5120], P('section', 'peer')
- mean_in: float32 [16, 2, 16, 5120], P('section', None, None, 'peer')
- mean_out: float32 [16, 2, 16, 5120], P('section', None, None, 'peer')
The draws below stay inside these ranges and needn't reach their ends.
Inputs may be any that keep to these rules, and one draw needn't show every extreme that they name: routes[s, p, q] is how many micro-batches peer p of section s sends to peer q of the next section; every row sums to 16; every column sums to at most 20, and in every section some column reaches 20; some entry of every section reaches 1.
All inputs are finite; a program needn't handle non-finite values.
Results may differ from the reference program's by a relative error of at most 0.015.
Values may be sent and summed in bfloat16 or wider, within the bound.
A program may use at most 64 MiB of HBM per device.

```python
import jax
import jax.numpy as jnp
from jax import lax

D = 5120
RANK = 16
LAYERS = 2
MB = 8
MICRO = 16
TOK_DEV = 128
PEERS = 32
SECTIONS = 16
PAIR = 1
CAP = 20


def one_table(key):
    hot_count = max(1, PEERS // 8)
    rest_total = PEERS * MICRO - hot_count * CAP
    others = PEERS - hot_count
    base_load = rest_total // others
    extra_load = rest_total % others
    ranks = jnp.arange(PEERS, dtype=jnp.int32)
    demand_by_rank = jnp.where(ranks < hot_count, CAP, base_load + (ranks - hot_count < extra_load).astype(jnp.int32))
    order = jax.random.permutation(jax.random.fold_in(key, 1), PEERS)
    demand = jnp.zeros((PEERS,), jnp.int32).at[order].set(demand_by_rank.astype(jnp.int32))
    noise_key = jax.random.fold_in(key, 2)

    def row_step(row, carry):
        table, remaining = carry

        def unit_step(unit, inner):
            counts, left = inner
            noise = jax.random.permutation(jax.random.fold_in(noise_key, row * MICRO + unit), PEERS).astype(jnp.int32)
            eligible = (counts < PAIR) & (left > 0)
            score = jnp.where(eligible, left * 4096 + noise, -1)
            chosen = lax.top_k(score, 1)[1][0]
            hit = (jnp.arange(PEERS, dtype=jnp.int32) == chosen).astype(jnp.int32)
            return (counts + hit, left - hit)
        counts, remaining = lax.fori_loop(0, MICRO, unit_step, (jnp.zeros((PEERS,), jnp.int32), remaining))
        table = lax.dynamic_update_slice(table, counts[None, :], (row, 0))
        return (table, remaining)
    table, remaining = lax.fori_loop(0, PEERS, row_step, (jnp.zeros((PEERS, PEERS), jnp.int32), demand))
    return table


def draw_routes(key, part):
    keys = jax.random.split(key, SECTIONS)
    return jax.vmap(one_table)(keys)


def level_of(rng, shape, shards, smallest, high):
    loudness = 1.0
    for dim, parts in shards:
        draws = jax.random.uniform(jax.random.fold_in(jax.random.fold_in(rng, 6), dim), (parts,), jnp.float32, smallest / len(shards), high / len(shards))
        loudness = loudness * jnp.repeat(jnp.exp(draws), shape[dim] // parts).reshape((-1,) + (1,) * (len(shape) - 1 - dim))
    return loudness


def normal_values(own_key, extent, scale, bound, cuts=(), held_as=jnp.bfloat16):
    array = jax.random.normal(own_key, extent, jnp.float32) * scale
    if len(cuts) > 0:
        array = level_of(own_key, extent, cuts, -0.22, 0.18) * array
    return jnp.clip(array, min=-bound, max=bound).astype(held_as)


def setup_inputs(seed: int = 0) -> dict:
    key_list = jax.random.split(jax.random.key(seed), 6)
    return {
        "inbox": normal_values(key_list[0], (SECTIONS, PEERS, TOK_DEV, D), 1.0, 6.0, ((0, 16), (1, 32))),
        "routes": draw_routes(jax.random.fold_in(key_list[5], 71), 0),
        "adapter_in": normal_values(key_list[2], (SECTIONS, LAYERS, RANK, D), D ** -0.5, 0.078125, ((0, 16),)),
        "adapter_out": normal_values(key_list[3], (SECTIONS, LAYERS, RANK, D), RANK ** -0.5, 1.5, ((0, 16),)),
        "returned": normal_values(key_list[4], (SECTIONS, PEERS, CAP * MB, D), 1.0, 6.0, ((0, 16), (1, 32))),
    }


epsilon = 1e-06

def inverse_rms(hidden):
    return lax.rsqrt(lax.optimization_barrier(jnp.mean(hidden * hidden, axis=-1, keepdims=True)) + epsilon)

def contract_last(left, right):
    return lax.dot_general(left, right, (((1,), (1,)), ((), ())), preferred_element_type=jnp.float32)

def contract_first(left, right):
    return lax.dot_general(left, right, (((0,), (0,)), ((), ())), preferred_element_type=jnp.float32)

def section_forward(inputs, weight_in, weight_out):
    hidden = inputs.astype(jnp.float32)
    for layer in range(weight_in.shape[0]):
        normed = (hidden * inverse_rms(hidden)).astype(jnp.bfloat16)
        lowered = contract_last(normed, weight_in[layer]).astype(jnp.bfloat16)
        hidden = hidden + jnp.dot(lowered, weight_out[layer], preferred_element_type=jnp.float32)
    return hidden.astype(jnp.bfloat16)

def section_backward(inputs, weight_in, weight_out, incoming):
    hidden = inputs.astype(jnp.float32)
    saved = []
    for layer in range(weight_in.shape[0]):
        saved.append(hidden)
        normed = (hidden * inverse_rms(hidden)).astype(jnp.bfloat16)
        lowered = contract_last(normed, weight_in[layer]).astype(jnp.bfloat16)
        hidden = hidden + jnp.dot(lowered, weight_out[layer], preferred_element_type=jnp.float32)
    grad = incoming.astype(jnp.float32)
    grads_in = []
    grads_out = []
    for layer in reversed(range(weight_in.shape[0])):
        hidden = saved[layer]
        scale = inverse_rms(hidden)
        plain = hidden * scale
        normed = plain.astype(jnp.bfloat16)
        lowered = contract_last(normed, weight_in[layer]).astype(jnp.bfloat16)
        grad_bf = grad.astype(jnp.bfloat16)
        grads_out.append(contract_first(lowered, grad_bf))
        back_low = contract_last(grad_bf, weight_out[layer]).astype(jnp.bfloat16)
        grads_in.append(contract_first(back_low, normed))
        if layer > 0:
            spread = jnp.dot(back_low, weight_in[layer], preferred_element_type=jnp.float32)
            grad = grad + scale * (spread - plain * lax.optimization_barrier(jnp.mean(spread * plain, axis=-1, keepdims=True)))
    return (jnp.stack(grads_in[::-1]), jnp.stack(grads_out[::-1]))

def slot_sources(counts):
    sent_end = jnp.cumsum(counts, axis=1)
    sent_start = sent_end - counts
    slot_start = jnp.cumsum(counts, axis=0) - counts
    slot_end = slot_start + counts
    positions = jnp.arange(CAP, dtype=jnp.int32)
    owner = lax.optimization_barrier(jnp.sum((slot_end.T[:, :, None] <= positions[None, None, :]).astype(jnp.int32), axis=1))
    valid = positions[None, :] < lax.optimization_barrier(jnp.sum(counts, axis=0))[:, None]
    owner = jnp.minimum(owner, PEERS - 1).astype(jnp.int32)
    offset = positions[None, :] - jnp.take_along_axis(slot_start.T, owner, axis=1)
    micro_index = jnp.take_along_axis(sent_start.T, owner, axis=1) + offset
    micro_index = jnp.where(valid, micro_index, 0)
    return ((owner * MICRO + micro_index).astype(jnp.int32), valid)

def send_targets(counts):
    sent_end = jnp.cumsum(counts, axis=1)
    sent_start = sent_end - counts
    slot_start = jnp.cumsum(counts, axis=0) - counts
    micro = jnp.arange(MICRO, dtype=jnp.int32)
    target = lax.optimization_barrier(jnp.sum((sent_end[:, None, :] <= micro[None, :, None]).astype(jnp.int32), axis=2)).astype(jnp.int32)
    offset = micro[None, :] - jnp.take_along_axis(sent_start, target, axis=1)
    slot = jnp.take_along_axis(slot_start, target, axis=1) + offset
    return (target, slot.astype(jnp.int32))

def reference(inbox, routes, adapter_in, adapter_out, returned):
    width = inbox.shape[-1]

    def forward_one(section_args):
        inputs, weight_in, weight_out = section_args
        return jax.vmap(section_forward, in_axes=(0, None, None))(inputs, weight_in, weight_out)
    outgoing = lax.map(forward_one, (inbox, adapter_in, adapter_out))

    def deliver(section_args):
        produced, counts = section_args
        sources, valid = slot_sources(counts)
        blocks = produced.reshape(PEERS * MICRO, MB, width)
        picked = blocks[sources]
        picked = jnp.where(valid[:, :, None, None], picked, jnp.zeros((), picked.dtype))
        return picked.reshape(PEERS, CAP * MB, width)
    handed = lax.map(deliver, (jnp.roll(outgoing, 1, axis=0), jnp.roll(routes, 1, axis=0)))

    def backward_one(section_args):
        inputs, weight_in, weight_out, slots_next, counts = section_args
        target, slot = send_targets(counts)
        arriving = slots_next.reshape(PEERS, CAP, MB, width)[target, slot]
        arriving = arriving.reshape(PEERS, MICRO * MB, width)
        terms_in, terms_out = jax.vmap(section_backward, in_axes=(0, None, None, 0))(inputs, weight_in, weight_out, arriving)
        return (lax.optimization_barrier(jnp.sum(terms_in, axis=0)) / PEERS, lax.optimization_barrier(jnp.sum(terms_out, axis=0)) / PEERS)
    mean_in, mean_out = lax.map(backward_one, (inbox, adapter_in, adapter_out, jnp.roll(returned, -1, axis=0), routes))
    return (handed, mean_in, mean_out)
```

```python
import jax
import jax.numpy as jnp
from jax import lax
from jax.experimental import pallas as pl
from jax.experimental.pallas import tpu as pltpu
from jax.sharding import PartitionSpec as P

MESH = pl.DeviceIdType.MESH
BF = jnp.bfloat16
F32 = jnp.float32

D = 5120
MB = 8
RANK = 16
SECTIONS = 16
PEERS = 32
ROWS_Y = 8
MICRO = 16
CAP = 20
TOK = CAP * MB
BLOCK = 32
CHUNK = 1024
WINDOW = 384
epsilon = 1e-06

STEPS = [(dy, dz, dc) for dy in (4, 3, 5, 2, 6, 1, 7, 0) for dz in (1, 0) for dc in (0, 1)]


def split_peer(peer):
    return peer // 16, (peer // 2) % ROWS_Y, peer % 2


def join_peer(z, y, c):
    return z * 16 + y * 2 + c


def route_kernel(
    pick, inbox, w_in, w_out, arrived, weights, staged, relay, s1, r1, s2, r2, sw, rw
):
    section = lax.axis_index("section")
    z, y, c = split_peer(lax.axis_index("peer"))
    ahead = (section + 1) % SECTIONS
    behind = (section + SECTIONS - 1) % SECTIONS
    in_plane = [(dy, dc) for dy in range(ROWS_Y) for dc in (0, 1) if dy or dc]

    barrier = pltpu.get_barrier_semaphore()
    for dz in (0, 1):
        pl.semaphore_signal(
            barrier,
            inc=1,
            device_id=(behind, join_peer((z + dz) % 2, y, c)),
            device_id_type=MESH,
        )
    for dy, dc in in_plane:
        pl.semaphore_signal(
            barrier,
            inc=1,
            device_id=(section, join_peer(z, (y + dy) % ROWS_Y, (c + dc) % 2)),
            device_id_type=MESH,
        )
    for i, (dy, dz, dc) in enumerate(STEPS):
        target = join_peer((z + dz) % 2, (y + dy) % ROWS_Y, (c + dc) % 2)
        staged[i] = inbox[pick[target]]
    pl.semaphore_wait(barrier, 2 + len(in_plane))

    def weight_hop(source):
        return pltpu.make_async_remote_copy(
            src_ref=source,
            dst_ref=weights.at[c],
            send_sem=sw.at[0],
            recv_sem=rw.at[0],
            device_id=(ahead, join_peer(z, y, c)),
            device_id_type=MESH,
        )

    def first_hop(i):
        return pltpu.make_async_remote_copy(
            src_ref=staged.at[i],
            dst_ref=relay.at[i],
            send_sem=s1.at[i],
            recv_sem=r1.at[i],
            device_id=(ahead, join_peer((z + STEPS[i][1]) % 2, y, c)),
            device_id_type=MESH,
        )

    def second_hop(i):
        dy, _, dc = STEPS[i]
        return pltpu.make_async_remote_copy(
            src_ref=relay.at[i],
            dst_ref=arrived.at[i],
            send_sem=s2.at[i],
            recv_sem=r2.at[i],
            device_id=(section, join_peer(z, (y + dy) % ROWS_Y, (c + dc) % 2)),
            device_id_type=MESH,
        )

    first = [first_hop(i) for i in range(len(STEPS))]
    second = [second_hop(i) if dy or dc else None for i, (dy, _, dc) in enumerate(STEPS)]
    for i in range(16):
        first[i].start()

    @pl.when(c == 0)
    def _():
        weight_hop(w_in).start()

    @pl.when(c == 1)
    def _():
        weight_hop(w_out).start()

    for i in range(16, len(STEPS)):
        first[i].start()

    share = pltpu.make_async_remote_copy(
        src_ref=weights.at[c],
        dst_ref=weights.at[c],
        send_sem=sw.at[1],
        recv_sem=rw.at[1],
        device_id=(section, join_peer(z, y, 1 - c)),
        device_id_type=MESH,
    )
    for i in range(len(STEPS)):
        first[i].wait_recv()
        if second[i] is None:
            arrived[i] = relay[i]
        else:
            second[i].start()
        if i == 23:
            weight_hop(w_in).wait_recv()
            share.start()
    for i in range(len(STEPS)):
        first[i].wait_send()
        if second[i] is not None:
            second[i].wait()
    weight_hop(w_in).wait_send()
    share.wait()


def route(pick, inbox, w_in, w_out):
    count = len(STEPS)
    slots = (count, MB, D)
    vmem = pl.BlockSpec(memory_space=pltpu.VMEM)
    return pl.pallas_call(
        route_kernel,
        out_shape=(
            jax.ShapeDtypeStruct(slots, BF),
            jax.ShapeDtypeStruct((2, 2, RANK, D), BF),
        ),
        in_specs=[pl.BlockSpec(memory_space=pltpu.SMEM), vmem, vmem, vmem],
        out_specs=(vmem, vmem),
        scratch_shapes=[
            pltpu.VMEM(slots, BF),
            pltpu.VMEM(slots, BF),
            pltpu.SemaphoreType.DMA((count,)),
            pltpu.SemaphoreType.DMA((count,)),
            pltpu.SemaphoreType.DMA((count,)),
            pltpu.SemaphoreType.DMA((count,)),
            pltpu.SemaphoreType.DMA((2,)),
            pltpu.SemaphoreType.DMA((2,)),
        ],
        compiler_params=pltpu.CompilerParams(
            collective_id=0, has_side_effects=True, vmem_limit_bytes=32 << 20
        ),
        name="route",
    )(pick, inbox, w_in, w_out)


def across(left, right):
    return lax.dot_general(left, right, (((1,), (1,)), ((), ())), preferred_element_type=F32)


def down(left, right):
    return lax.dot_general(left, right, (((0,), (0,)), ((), ())), preferred_element_type=F32)


def along(left, right):
    return jnp.dot(left, right, preferred_element_type=F32)


def mean_of(total):
    return jnp.sum(total, axis=-1, keepdims=True) / D


def section_kernel(
    source, taken, arrived, returned, weights, handed, terms, hid, n0, n1, g1, l0, l1, b0, b1
):
    pieces = [pl.ds(k, CHUNK) for k in range(0, D, CHUNK)]

    def block(step, carry):
        rows = pl.ds(pl.multiple_of(step * BLOCK, BLOCK), BLOCK)
        square = jnp.zeros((BLOCK, 1), F32)
        for piece in pieces:
            parts = []
            for k in range(BLOCK // MB):
                slot = step * (BLOCK // MB) + k
                part = arrived[source[slot], :, piece].astype(F32)
                parts.append(jnp.where(taken[slot] > 0, part, 0.0))
            x = jnp.concatenate(parts, axis=0)
            hid[:, piece] = x
            square += jnp.sum(x * x, axis=-1, keepdims=True)
        scale0 = lax.rsqrt(square / D + epsilon)
        low = jnp.zeros((BLOCK, RANK), F32)
        for piece in pieces:
            normed = (hid[:, piece] * scale0).astype(BF)
            n0[rows, piece] = normed
            low += across(normed, weights[0, 0, :, piece])
        low0 = low.astype(BF)
        l0[rows, :] = low0
        square = jnp.zeros((BLOCK, 1), F32)
        for piece in pieces:
            x = hid[:, piece] + along(low0, weights[1, 0, :, piece])
            hid[:, piece] = x
            square += jnp.sum(x * x, axis=-1, keepdims=True)
        scale1 = lax.rsqrt(square / D + epsilon)
        low = jnp.zeros((BLOCK, RANK), F32)
        back = jnp.zeros((BLOCK, RANK), F32)
        for piece in pieces:
            normed = (hid[:, piece] * scale1).astype(BF)
            n1[rows, piece] = normed
            low += across(normed, weights[0, 1, :, piece])
            back += across(returned[rows, piece], weights[1, 1, :, piece])
        low1 = low.astype(BF)
        back1 = back.astype(BF)
        l1[rows, :] = low1
        b1[rows, :] = back1
        both = jnp.zeros((BLOCK, 1), F32)
        for piece in pieces:
            x = hid[:, piece]
            handed[rows, piece] = (x + along(low1, weights[1, 1, :, piece])).astype(BF)
            spread = along(back1, weights[0, 1, :, piece])
            both += jnp.sum(spread * (x * scale1), axis=-1, keepdims=True)
        both = both / D
        back = jnp.zeros((BLOCK, RANK), F32)
        for piece in pieces:
            plain = hid[:, piece] * scale1
            spread = along(back1, weights[0, 1, :, piece])
            grad = returned[rows, piece].astype(F32) + scale1 * (spread - plain * both)
            grad = grad.astype(BF)
            g1[rows, piece] = grad
            back += across(grad, weights[1, 0, :, piece])
        b0[rows, :] = back.astype(BF)
        return carry

    lax.fori_loop(0, TOK // BLOCK, block, 0)
    for piece in pieces:
        terms[0:16, piece] = down(b0[...], n0[:, piece])
        terms[16:32, piece] = down(b1[...], n1[:, piece])
        terms[32:48, piece] = down(l0[...], g1[:, piece])
        terms[48:64, piece] = down(l1[...], returned[:, piece])


def section_step(source, taken, arrived, returned, weights):
    vmem = pl.BlockSpec(memory_space=pltpu.VMEM)
    smem = pl.BlockSpec(memory_space=pltpu.SMEM)
    return pl.pallas_call(
        section_kernel,
        out_shape=(
            jax.ShapeDtypeStruct((TOK, D), BF),
            jax.ShapeDtypeStruct((4 * RANK, D), F32),
        ),
        in_specs=[smem, smem, vmem, vmem, vmem],
        out_specs=(vmem, vmem),
        scratch_shapes=[
            pltpu.VMEM((BLOCK, D), F32),
            pltpu.VMEM((TOK, D), BF),
            pltpu.VMEM((TOK, D), BF),
            pltpu.VMEM((TOK, D), BF),
            pltpu.VMEM((TOK, RANK), BF),
            pltpu.VMEM((TOK, RANK), BF),
            pltpu.VMEM((TOK, RANK), BF),
            pltpu.VMEM((TOK, RANK), BF),
        ],
        compiler_params=pltpu.CompilerParams(vmem_limit_bytes=40 << 20),
        name="section_step",
    )(source, taken, arrived, returned, weights)


HALF = 2 * RANK
SPREAD = [(dy, dz) for dy in (4, 3, 5, 2, 6, 1, 7, 0) for dz in (1, 0)]


def reduce_kernel(terms, total, half, other_half, summed, landed, own, other, ss, rs, sc, rc):
    section = lax.axis_index("section")
    z, y, c = split_peer(lax.axis_index("peer"))
    ahead = (section + 1) % SECTIONS
    behind = (section + SECTIONS - 1) % SECTIONS
    partner = (section, join_peer(z, y, 1 - c))
    mine = pl.ds(pl.multiple_of(c * HALF, HALF), HALF)
    theirs = pl.ds(pl.multiple_of((1 - c) * HALF, HALF), HALF)

    barrier = pltpu.get_barrier_semaphore()
    pl.semaphore_signal(barrier, inc=1, device_id=partner, device_id_type=MESH)
    for dy, dz in SPREAD:
        pl.semaphore_signal(
            barrier,
            inc=1,
            device_id=(ahead, join_peer((z + dz) % 2, (y + dy) % ROWS_Y, c)),
            device_id_type=MESH,
        )
    half[...] = terms[theirs, :].astype(BF)
    pl.semaphore_wait(barrier, 1 + len(SPREAD))

    to_core = pltpu.make_async_remote_copy(
        src_ref=half,
        dst_ref=other_half,
        send_sem=sc.at[0],
        recv_sem=rc.at[0],
        device_id=partner,
        device_id_type=MESH,
    )
    to_core.start()
    to_core.wait()
    summed[...] = (terms[mine, :] + other_half[...].astype(F32)).astype(BF)
    copies = []
    for i, (dy, dz) in enumerate(SPREAD):
        chip_z, chip_y = (z + dz) % 2, (y + dy) % ROWS_Y
        start = pl.multiple_of(128 * ((5 * (chip_z * ROWS_Y + chip_y)) // 2), 128)
        copy = pltpu.make_async_remote_copy(
            src_ref=summed.at[:, pl.ds(start, WINDOW)],
            dst_ref=landed.at[i],
            send_sem=ss.at[i],
            recv_sem=rs.at[i],
            device_id=(behind, join_peer(chip_z, chip_y, c)),
            device_id_type=MESH,
        )
        copy.start()
        copies.append(copy)
    for copy in copies:
        copy.wait()
    own[...] = jnp.sum(landed[...].astype(F32), axis=0)
    back = pltpu.make_async_remote_copy(
        src_ref=own,
        dst_ref=other,
        send_sem=sc.at[1],
        recv_sem=rc.at[1],
        device_id=partner,
        device_id_type=MESH,
    )
    back.start()
    back.wait()
    total[mine, :] = own[...] / PEERS
    total[theirs, :] = other[...] / PEERS


def reduce_terms(terms):
    vmem = pl.BlockSpec(memory_space=pltpu.VMEM)
    count = len(SPREAD)
    return pl.pallas_call(
        reduce_kernel,
        out_shape=jax.ShapeDtypeStruct((2 * HALF, WINDOW), F32),
        in_specs=[vmem],
        out_specs=vmem,
        scratch_shapes=[
            pltpu.VMEM((HALF, D), BF),
            pltpu.VMEM((HALF, D), BF),
            pltpu.VMEM((HALF, D), BF),
            pltpu.VMEM((count, HALF, WINDOW), BF),
            pltpu.VMEM((HALF, WINDOW), F32),
            pltpu.VMEM((HALF, WINDOW), F32),
            pltpu.SemaphoreType.DMA((count,)),
            pltpu.SemaphoreType.DMA((count,)),
            pltpu.SemaphoreType.DMA((2,)),
            pltpu.SemaphoreType.DMA((2,)),
        ],
        compiler_params=pltpu.CompilerParams(
            collective_id=1, has_side_effects=True, vmem_limit_bytes=32 << 20
        ),
        name="reduce_terms",
    )(terms)


def tables(routes, section, peer):
    row = lax.dynamic_index_in_dim(
        lax.dynamic_index_in_dim(routes, section, 0, keepdims=False), peer, 0, keepdims=False
    )
    behind = (section + SECTIONS - 1) % SECTIONS
    column = lax.dynamic_index_in_dim(
        lax.dynamic_index_in_dim(routes, behind, 0, keepdims=False), peer, 1, keepdims=False
    )
    index = jnp.arange(PEERS, dtype=jnp.int32)
    before = index[None, :] < index[:, None]
    pick = jnp.minimum(jnp.sum(jnp.where(before, row[None, :], 0), axis=1), MICRO - 1)
    slot = jnp.sum(jnp.where(before, column[None, :], 0), axis=1)
    z, y, c = split_peer(peer)
    from_z, from_y, from_c = split_peer(index)
    turn = (y - from_y + ROWS_Y) % ROWS_Y
    place = jnp.sum(
        jnp.where(
            turn[:, None] == jnp.asarray([4, 3, 5, 2, 6, 1, 7, 0], jnp.int32)[None, :],
            jnp.arange(ROWS_Y, dtype=jnp.int32)[None, :],
            0,
        ),
        axis=1,
    )
    step = place * 4 + jnp.where(from_z == z, 2, 0) + jnp.where(from_c == c, 0, 1)
    here = (jnp.arange(CAP, dtype=jnp.int32)[:, None] == slot[None, :]) & (column[None, :] > 0)
    source = jnp.sum(jnp.where(here, step[None, :], 0), axis=1)
    taken = jnp.sum(here.astype(jnp.int32), axis=1)
    return pick, source, taken


def shards(inbox, routes, adapter_in, adapter_out, returned):
    section = lax.axis_index("section")
    peer = lax.axis_index("peer")
    pick, source, taken = tables(routes, section, peer)
    arrived, weights = route(
        pick, inbox.reshape(MICRO, MB, D), adapter_in[0], adapter_out[0]
    )
    handed, terms = section_step(source, taken, arrived, returned[0, 0], weights)
    total = reduce_terms(terms)
    start = (peer // 2 % 2) * 64 + (peer % 2) * 160
    own = lax.dynamic_slice_in_dim(total, start, D // PEERS, axis=1).reshape(2, 2, RANK, D // PEERS)
    return handed[None, None], own[0][None], own[1][None]


def solution(mesh):
    return jax.shard_map(
        shards,
        mesh=mesh,
        in_specs=(
            P("section", "peer", None, None),
            P(),
            P("section", None, None, None),
            P("section", None, None, None),
            P("section", "peer", None, None),
        ),
        out_specs=(
            P("section", "peer", None, None),
            P("section", None, None, "peer"),
            P("section", None, None, "peer"),
        ),
        check_vma=False,
    )
```

```python
import jax
import jax.numpy as jnp
from jax import lax
from jax.experimental import pallas as pl
from jax.experimental.pallas import tpu as pltpu
from jax.sharding import PartitionSpec as P

MESH = pl.DeviceIdType.MESH
BF = jnp.bfloat16
F32 = jnp.float32

D = 5120
MB = 8
RANK = 16
SECTIONS = 16
PEERS = 32
ROWS_Y = 8
MICRO = 16
CAP = 20
TOK = CAP * MB
BLOCK = 32
CHUNK = 1024
WINDOW = 384
epsilon = 1e-06

SLOTS = [(dy, dc) for dy in (4, 3, 5, 2, 6, 1, 7, 0) for dc in (0, 1)]
FAR = len(SLOTS)
SPLIT = 4
LAG = 4


def place_of(section, peer):
    z = (peer // 16) * 4 + section // 4
    return section % 4, (peer // 2) % ROWS_Y, z, peer % 2


def device_at(x, y, z, c):
    z = (z + 8) % 8
    return (z % 4) * 4 + (x + 4) % 4, (z // 4) * 16 + ((y + ROWS_Y) % ROWS_Y) * 2 + c


def route_kernel(
    pick, inbox, w_in, w_out, arrived, weights, mine, staged, relay, middle, load, s1, r1, s2, r2, s3, s4, r3, sw, rw
):
    x, y, z, c = place_of(lax.axis_index("section"), lax.axis_index("peer"))
    leaving, entering = x == 3, x == 0
    shift_out, shift_in = jnp.where(leaving, 1, 0), jnp.where(entering, 1, 0)
    in_plane = [(dy, dc) for dy in range(ROWS_Y) for dc in (0, 1) if dy or dc]

    fetch = pltpu.make_async_copy(inbox, mine, load)
    fetch.start()
    barrier = pltpu.get_barrier_semaphore()

    def greet(*where):
        pl.semaphore_signal(barrier, inc=1, device_id=device_at(*where), device_id_type=MESH)

    greet(x - 1, y, z - shift_in, c)
    greet(x - 1, y, z - shift_in - 4, c)

    @pl.when(entering)
    def _():
        greet(x - 1, y, z - 3, c)
        greet(x, y, z - 2, c)

    for dy, dc in in_plane:
        greet(x, y + dy, z, (c + dc) % 2)
    fetch.wait()
    for k, (dy, dc) in enumerate(SLOTS):
        for far in (1, 0):
            target = device_at(x + 1, y + dy, z + shift_out + 4 * far, (c + dc) % 2)[1]
            staged[k + FAR * (1 - far)] = mine[pick[target]]
    greeted = 2 + len(in_plane) + shift_out + shift_in
    pl.semaphore_wait(barrier, greeted)

    def send(source, target, send_sem, recv_sem, *where):
        return pltpu.make_async_remote_copy(
            src_ref=source,
            dst_ref=target,
            send_sem=send_sem,
            recv_sem=recv_sem,
            device_id=device_at(*where),
            device_id_type=MESH,
        )

    def weight_hop(source):
        return send(source, weights.at[c], sw.at[0], rw.at[0], x + 1, y, z + shift_out, c)

    near, far, outward, onward, final = [], [], [], [], []
    for k in range(FAR):
        far.append(
            send(
                staged.at[k], relay.at[k], s2.at[k], r2.at[k],
                x + 1, y, z + shift_out + 4, c,
            )
        )
        near.append(
            send(
                staged.at[FAR + k], relay.at[FAR + k], s2.at[FAR + k], r2.at[FAR + k],
                x + 1, y, z + shift_out, c,
            )
        )
    for k in range(SPLIT):
        outward.append(
            send(staged.at[k], middle.at[k], s1.at[k], r1.at[k], x + 1, y, z + 3, c)
        )
        onward.append(send(middle.at[k], relay.at[k], s3.at[k], r2.at[k], x, y, z + 2, c))
    for i in range(2 * FAR):
        dy, dc = SLOTS[i % FAR]
        if dy or dc:
            final.append(
                send(
                    relay.at[i], arrived.at[i], s4.at[i], r3.at[i],
                    x, y + dy, z, (c + dc) % 2,
                )
            )
        else:
            final.append(None)

    def pass_on(i):
        if final[i] is None:
            arrived[i] = relay[i]
        else:
            final[i].start()

    @pl.when(leaving)
    def _():
        for k in range(SPLIT):
            outward[k].start()

    for k in range(FAR):
        if k < SPLIT:

            @pl.when(jnp.logical_not(leaving))
            def _():
                far[k].start()
        else:
            far[k].start()
        near[k].start()
        if k == FAR // 2:

            @pl.when(c == 0)
            def _():
                weight_hop(w_in).start()

            @pl.when(c == 1)
            def _():
                weight_hop(w_out).start()

    share = send(weights.at[c], weights.at[c], sw.at[1], rw.at[1], x, y, z, 1 - c)
    order = list(range(SPLIT, FAR))
    order = order[:SPLIT] + list(range(SPLIT)) + order[SPLIT:]
    for t in range(FAR + LAG):
        if t < FAR:
            near[t].wait_recv()
            pass_on(FAR + t)
        if t < SPLIT:

            @pl.when(entering)
            def _():
                outward[t].wait_recv()
                onward[t].start()
        if t == FAR - 2:
            weight_hop(w_in).wait_recv()
            share.start()
        if t >= LAG:
            far[order[t - LAG]].wait_recv()
            pass_on(order[t - LAG])
    for k in range(FAR):
        near[k].wait_send()
        if k >= SPLIT:
            far[k].wait_send()

    @pl.when(leaving)
    def _():
        for copy in outward:
            copy.wait_send()

    @pl.when(jnp.logical_not(leaving))
    def _():
        for copy in far[:SPLIT]:
            copy.wait_send()

    @pl.when(entering)
    def _():
        for copy in onward:
            copy.wait_send()

    for copy in final:
        if copy is not None:
            copy.wait()
    weight_hop(w_in).wait_send()
    share.wait()


def route(pick, inbox, w_in, w_out):
    slots = (2 * FAR, MB, D)
    vmem = pl.BlockSpec(memory_space=pltpu.VMEM)
    anywhere = pl.BlockSpec(memory_space=pl.ANY)
    dma = pltpu.SemaphoreType.DMA
    return pl.pallas_call(
        route_kernel,
        out_shape=(
            jax.ShapeDtypeStruct(slots, BF),
            jax.ShapeDtypeStruct((2, 2, RANK, D), BF),
        ),
        in_specs=[pl.BlockSpec(memory_space=pltpu.SMEM), anywhere, anywhere, anywhere],
        out_specs=(vmem, vmem),
        scratch_shapes=[
            pltpu.VMEM((MICRO, MB, D), BF),
            pltpu.VMEM(slots, BF),
            pltpu.VMEM(slots, BF),
            pltpu.VMEM((SPLIT, MB, D), BF),
            dma(()),
            dma((SPLIT,)),
            dma((SPLIT,)),
            dma((2 * FAR,)),
            dma((2 * FAR,)),
            dma((SPLIT,)),
            dma((2 * FAR,)),
            dma((2 * FAR,)),
            dma((2,)),
            dma((2,)),
        ],
        compiler_params=pltpu.CompilerParams(
            collective_id=0, has_side_effects=True, vmem_limit_bytes=32 << 20
        ),
        name="route",
    )(pick, inbox, w_in, w_out)


def across(left, right):
    return lax.dot_general(left, right, (((1,), (1,)), ((), ())), preferred_element_type=F32)


def down(left, right):
    return lax.dot_general(left, right, (((0,), (0,)), ((), ())), preferred_element_type=F32)


def along(left, right):
    return jnp.dot(left, right, preferred_element_type=F32)


def mean_of(total):
    return jnp.sum(total, axis=-1, keepdims=True) / D


def section_kernel(
    source, taken, arrived, returned, weights, handed, terms, hid, n0, n1, g1, l0, l1, b0, b1
):
    pieces = [pl.ds(k, CHUNK) for k in range(0, D, CHUNK)]

    def block(step, carry):
        rows = pl.ds(pl.multiple_of(step * BLOCK, BLOCK), BLOCK)
        square = jnp.zeros((BLOCK, 1), F32)
        for piece in pieces:
            parts = []
            for k in range(BLOCK // MB):
                slot = step * (BLOCK // MB) + k
                part = arrived[source[slot], :, piece].astype(F32)
                parts.append(jnp.where(taken[slot] > 0, part, 0.0))
            x = jnp.concatenate(parts, axis=0)
            hid[:, piece] = x
            square += jnp.sum(x * x, axis=-1, keepdims=True)
        scale0 = lax.rsqrt(square / D + epsilon)
        low = jnp.zeros((BLOCK, RANK), F32)
        for piece in pieces:
            normed = (hid[:, piece] * scale0).astype(BF)
            n0[rows, piece] = normed
            low += across(normed, weights[0, 0, :, piece])
        low0 = low.astype(BF)
        l0[rows, :] = low0
        square = jnp.zeros((BLOCK, 1), F32)
        for piece in pieces:
            x = hid[:, piece] + along(low0, weights[1, 0, :, piece])
            hid[:, piece] = x
            square += jnp.sum(x * x, axis=-1, keepdims=True)
        scale1 = lax.rsqrt(square / D + epsilon)
        low = jnp.zeros((BLOCK, RANK), F32)
        back = jnp.zeros((BLOCK, RANK), F32)
        for piece in pieces:
            normed = (hid[:, piece] * scale1).astype(BF)
            n1[rows, piece] = normed
            low += across(normed, weights[0, 1, :, piece])
            back += across(returned[rows, piece], weights[1, 1, :, piece])
        low1 = low.astype(BF)
        back1 = back.astype(BF)
        l1[rows, :] = low1
        b1[rows, :] = back1
        both = jnp.zeros((BLOCK, 1), F32)
        for piece in pieces:
            x = hid[:, piece]
            handed[rows, piece] = (x + along(low1, weights[1, 1, :, piece])).astype(BF)
            spread = along(back1, weights[0, 1, :, piece])
            both += jnp.sum(spread * (x * scale1), axis=-1, keepdims=True)
        both = both / D
        back = jnp.zeros((BLOCK, RANK), F32)
        for piece in pieces:
            plain = hid[:, piece] * scale1
            spread = along(back1, weights[0, 1, :, piece])
            grad = returned[rows, piece].astype(F32) + scale1 * (spread - plain * both)
            grad = grad.astype(BF)
            g1[rows, piece] = grad
            back += across(grad, weights[1, 0, :, piece])
        b0[rows, :] = back.astype(BF)
        return carry

    lax.fori_loop(0, TOK // BLOCK, block, 0)
    for piece in pieces:
        terms[0:16, piece] = down(b0[...], n0[:, piece])
        terms[16:32, piece] = down(b1[...], n1[:, piece])
        terms[32:48, piece] = down(l0[...], g1[:, piece])
        terms[48:64, piece] = down(l1[...], returned[:, piece])


def section_step(source, taken, arrived, returned, weights):
    vmem = pl.BlockSpec(memory_space=pltpu.VMEM)
    smem = pl.BlockSpec(memory_space=pltpu.SMEM)
    return pl.pallas_call(
        section_kernel,
        out_shape=(
            jax.ShapeDtypeStruct((TOK, D), BF),
            jax.ShapeDtypeStruct((4 * RANK, D), F32),
        ),
        in_specs=[smem, smem, vmem, vmem, vmem],
        out_specs=(vmem, vmem),
        scratch_shapes=[
            pltpu.VMEM((BLOCK, D), F32),
            pltpu.VMEM((TOK, D), BF),
            pltpu.VMEM((TOK, D), BF),
            pltpu.VMEM((TOK, D), BF),
            pltpu.VMEM((TOK, RANK), BF),
            pltpu.VMEM((TOK, RANK), BF),
            pltpu.VMEM((TOK, RANK), BF),
            pltpu.VMEM((TOK, RANK), BF),
        ],
        compiler_params=pltpu.CompilerParams(vmem_limit_bytes=40 << 20),
        name="section_step",
    )(source, taken, arrived, returned, weights)


def split_peer(peer):
    return peer // 16, (peer // 2) % ROWS_Y, peer % 2


def join_peer(z, y, c):
    return z * 16 + y * 2 + c


HALF = 2 * RANK
SPREAD = [(dy, dz) for dy in (4, 3, 5, 2, 6, 1, 7, 0) for dz in (1, 0)]


def reduce_kernel(terms, total, half, other_half, summed, landed, own, other, ss, rs, sc, rc):
    section = lax.axis_index("section")
    z, y, c = split_peer(lax.axis_index("peer"))
    ahead = (section + 1) % SECTIONS
    behind = (section + SECTIONS - 1) % SECTIONS
    partner = (section, join_peer(z, y, 1 - c))
    mine = pl.ds(pl.multiple_of(c * HALF, HALF), HALF)
    theirs = pl.ds(pl.multiple_of((1 - c) * HALF, HALF), HALF)

    barrier = pltpu.get_barrier_semaphore()
    pl.semaphore_signal(barrier, inc=1, device_id=partner, device_id_type=MESH)
    for dy, dz in SPREAD:
        pl.semaphore_signal(
            barrier,
            inc=1,
            device_id=(ahead, join_peer((z + dz) % 2, (y + dy) % ROWS_Y, c)),
            device_id_type=MESH,
        )
    half[...] = terms[theirs, :].astype(BF)
    pl.semaphore_wait(barrier, 1 + len(SPREAD))

    to_core = pltpu.make_async_remote_copy(
        src_ref=half,
        dst_ref=other_half,
        send_sem=sc.at[0],
        recv_sem=rc.at[0],
        device_id=partner,
        device_id_type=MESH,
    )
    to_core.start()
    to_core.wait()
    summed[...] = (terms[mine, :] + other_half[...].astype(F32)).astype(BF)
    copies = []
    for i, (dy, dz) in enumerate(SPREAD):
        chip_z, chip_y = (z + dz) % 2, (y + dy) % ROWS_Y
        start = pl.multiple_of(128 * ((5 * (chip_z * ROWS_Y + chip_y)) // 2), 128)
        copy = pltpu.make_async_remote_copy(
            src_ref=summed.at[:, pl.ds(start, WINDOW)],
            dst_ref=landed.at[i],
            send_sem=ss.at[i],
            recv_sem=rs.at[i],
            device_id=(behind, join_peer(chip_z, chip_y, c)),
            device_id_type=MESH,
        )
        copy.start()
        copies.append(copy)
    for copy in copies:
        copy.wait()
    own[...] = jnp.sum(landed[...].astype(F32), axis=0)
    back = pltpu.make_async_remote_copy(
        src_ref=own,
        dst_ref=other,
        send_sem=sc.at[1],
        recv_sem=rc.at[1],
        device_id=partner,
        device_id_type=MESH,
    )
    back.start()
    back.wait()
    total[mine, :] = own[...] / PEERS
    total[theirs, :] = other[...] / PEERS


def reduce_terms(terms):
    vmem = pl.BlockSpec(memory_space=pltpu.VMEM)
    count = len(SPREAD)
    return pl.pallas_call(
        reduce_kernel,
        out_shape=jax.ShapeDtypeStruct((2 * HALF, WINDOW), F32),
        in_specs=[vmem],
        out_specs=vmem,
        scratch_shapes=[
            pltpu.VMEM((HALF, D), BF),
            pltpu.VMEM((HALF, D), BF),
            pltpu.VMEM((HALF, D), BF),
            pltpu.VMEM((count, HALF, WINDOW), BF),
            pltpu.VMEM((HALF, WINDOW), F32),
            pltpu.VMEM((HALF, WINDOW), F32),
            pltpu.SemaphoreType.DMA((count,)),
            pltpu.SemaphoreType.DMA((count,)),
            pltpu.SemaphoreType.DMA((2,)),
            pltpu.SemaphoreType.DMA((2,)),
        ],
        compiler_params=pltpu.CompilerParams(
            collective_id=1, has_side_effects=True, vmem_limit_bytes=32 << 20
        ),
        name="reduce_terms",
    )(terms)


def tables(routes, section, peer):
    row = lax.dynamic_index_in_dim(
        lax.dynamic_index_in_dim(routes, section, 0, keepdims=False), peer, 0, keepdims=False
    )
    behind = (section + SECTIONS - 1) % SECTIONS
    column = lax.dynamic_index_in_dim(
        lax.dynamic_index_in_dim(routes, behind, 0, keepdims=False), peer, 1, keepdims=False
    )
    index = jnp.arange(PEERS, dtype=jnp.int32)
    before = index[None, :] < index[:, None]
    pick = jnp.minimum(jnp.sum(jnp.where(before, row[None, :], 0), axis=1), MICRO - 1)
    slot = jnp.sum(jnp.where(before, column[None, :], 0), axis=1)
    x, y, z, c = place_of(section, peer)
    near_z = (z + 8 - jnp.where(x == 0, 1, 0)) % 8 // 4
    from_z, from_y, from_c = split_peer(index)
    turn = (y - from_y + ROWS_Y) % ROWS_Y
    order = jnp.asarray([dy for dy, dc in SLOTS if dc == 0], jnp.int32)
    place = jnp.sum(
        jnp.where(
            turn[:, None] == order[None, :], jnp.arange(ROWS_Y, dtype=jnp.int32)[None, :], 0
        ),
        axis=1,
    )
    step = place * 2 + jnp.where(from_z == near_z, FAR, 0) + jnp.where(from_c == c, 0, 1)
    here = (jnp.arange(CAP, dtype=jnp.int32)[:, None] == slot[None, :]) & (column[None, :] > 0)
    source = jnp.sum(jnp.where(here, step[None, :], 0), axis=1)
    taken = jnp.sum(here.astype(jnp.int32), axis=1)
    return pick, source, taken


def shards(inbox, routes, adapter_in, adapter_out, returned):
    section = lax.axis_index("section")
    peer = lax.axis_index("peer")
    pick, source, taken = tables(routes, section, peer)
    arrived, weights = route(
        pick, inbox.reshape(MICRO, MB, D), adapter_in[0], adapter_out[0]
    )
    handed, terms = section_step(source, taken, arrived, returned[0, 0], weights)
    total = reduce_terms(terms)
    start = (peer // 2 % 2) * 64 + (peer % 2) * 160
    own = lax.dynamic_slice_in_dim(total, start, D // PEERS, axis=1).reshape(2, 2, RANK, D // PEERS)
    return handed[None, None], own[0][None], own[1][None]


def solution(mesh):
    return jax.shard_map(
        shards,
        mesh=mesh,
        in_specs=(
            P("section", "peer", None, None),
            P(),
            P("section", None, None, None),
            P("section", None, None, None),
            P("section", "peer", None, None),
        ),
        out_specs=(
            P("section", "peer", None, None),
            P("section", None, None, "peer"),
            P("section", None, None, "peer"),
        ),
        check_vma=False,
    )
```

```python
import jax
import jax.numpy as jnp
from jax import lax
from jax.experimental import pallas as pl
from jax.experimental.pallas import tpu as pltpu
from jax.sharding import PartitionSpec as P

MESH = pl.DeviceIdType.MESH
BF = jnp.bfloat16
F32 = jnp.float32

D = 5120
MB = 8
RANK = 16
SECTIONS = 16
PEERS = 32
ROWS_Y = 8
MICRO = 16
CAP = 20
TOK = CAP * MB
BLOCK = 160
CHUNK = 256
WINDOW = 384
epsilon = 1e-06

SLOTS = [(dy, dc) for dy in (4, 3, 5, 2, 6, 1, 7, 0) for dc in (0, 1)]
FAR = len(SLOTS)
SPLIT = 4
LAG = 4


def place_of(section, peer):
    z = (peer // 16) * 4 + section // 4
    return section % 4, (peer // 2) % ROWS_Y, z, peer % 2


def device_at(x, y, z, c):
    z = (z + 8) % 8
    return (z % 4) * 4 + (x + 4) % 4, (z // 4) * 16 + ((y + ROWS_Y) % ROWS_Y) * 2 + c


def route_kernel(
    pick, inbox, w_in, w_out, arrived, weights, mine, staged, relay, middle, load, s1, r1, s2, r2, s3, s4, r3, sw, rw
):
    x, y, z, c = place_of(lax.axis_index("section"), lax.axis_index("peer"))
    leaving, entering = x == 3, x == 0
    shift_out, shift_in = jnp.where(leaving, 1, 0), jnp.where(entering, 1, 0)
    in_plane = [(dy, dc) for dy in range(ROWS_Y) for dc in (0, 1) if dy or dc]

    fetch = pltpu.make_async_copy(inbox, mine, load)
    fetch.start()
    barrier = pltpu.get_barrier_semaphore()

    def greet(*where):
        pl.semaphore_signal(barrier, inc=1, device_id=device_at(*where), device_id_type=MESH)

    greet(x - 1, y, z - shift_in, c)
    greet(x - 1, y, z - shift_in - 4, c)

    @pl.when(entering)
    def _():
        greet(x - 1, y, z - 3, c)
        greet(x, y, z - 2, c)

    for dy, dc in in_plane:
        greet(x, y + dy, z, (c + dc) % 2)
    fetch.wait()
    for k, (dy, dc) in enumerate(SLOTS):
        for far in (1, 0):
            target = device_at(x + 1, y + dy, z + shift_out + 4 * far, (c + dc) % 2)[1]
            staged[k + FAR * (1 - far)] = mine[pick[target]]
    greeted = 2 + len(in_plane) + shift_out + shift_in
    pl.semaphore_wait(barrier, greeted)

    def send(source, target, send_sem, recv_sem, *where):
        return pltpu.make_async_remote_copy(
            src_ref=source,
            dst_ref=target,
            send_sem=send_sem,
            recv_sem=recv_sem,
            device_id=device_at(*where),
            device_id_type=MESH,
        )

    def weight_hop(source):
        return send(source, weights.at[c], sw.at[0], rw.at[0], x + 1, y, z + shift_out, c)

    near, far, outward, onward, final = [], [], [], [], []
    for k in range(FAR):
        far.append(
            send(
                staged.at[k], relay.at[k], s2.at[k], r2.at[k],
                x + 1, y, z + shift_out + 4, c,
            )
        )
        near.append(
            send(
                staged.at[FAR + k], relay.at[FAR + k], s2.at[FAR + k], r2.at[FAR + k],
                x + 1, y, z + shift_out, c,
            )
        )
    for k in range(SPLIT):
        outward.append(
            send(staged.at[k], middle.at[k], s1.at[k], r1.at[k], x + 1, y, z + 3, c)
        )
        onward.append(send(middle.at[k], relay.at[k], s3.at[k], r2.at[k], x, y, z + 2, c))
    for i in range(2 * FAR):
        dy, dc = SLOTS[i % FAR]
        if dy or dc:
            final.append(
                send(
                    relay.at[i], arrived.at[i], s4.at[i], r3.at[i],
                    x, y + dy, z, (c + dc) % 2,
                )
            )
        else:
            final.append(None)

    def pass_on(i):
        if final[i] is None:
            arrived[i] = relay[i]
        else:
            final[i].start()

    for k in range(FAR):
        if k < SPLIT:

            @pl.when(jnp.logical_not(leaving))
            def _():
                far[k].start()
        else:
            far[k].start()
        near[k].start()
        if k < SPLIT:

            @pl.when(leaving)
            def _():
                outward[k].start()

        if k == FAR - 3:

            @pl.when(c == 0)
            def _():
                weight_hop(w_in).start()

            @pl.when(c == 1)
            def _():
                weight_hop(w_out).start()

    share = send(weights.at[c], weights.at[c], sw.at[1], rw.at[1], x, y, z, 1 - c)
    order = list(range(SPLIT, FAR))
    order = order[:SPLIT] + list(range(SPLIT)) + order[SPLIT:]
    for t in range(FAR + LAG):
        if t < FAR:
            near[t].wait_recv()
            pass_on(FAR + t)
        if t < SPLIT:

            @pl.when(entering)
            def _():
                outward[t].wait_recv()
                onward[t].start()
        if t == FAR:
            weight_hop(w_in).wait_recv()
            share.start()
        if t >= LAG:
            far[order[t - LAG]].wait_recv()
            pass_on(order[t - LAG])
    for k in range(FAR):
        near[k].wait_send()
        if k >= SPLIT:
            far[k].wait_send()

    @pl.when(leaving)
    def _():
        for copy in outward:
            copy.wait_send()

    @pl.when(jnp.logical_not(leaving))
    def _():
        for copy in far[:SPLIT]:
            copy.wait_send()

    @pl.when(entering)
    def _():
        for copy in onward:
            copy.wait_send()

    for copy in final:
        if copy is not None:
            copy.wait()
    weight_hop(w_in).wait_send()
    share.wait()


def route(pick, inbox, w_in, w_out):
    slots = (2 * FAR, MB, D)
    vmem = pl.BlockSpec(memory_space=pltpu.VMEM)
    anywhere = pl.BlockSpec(memory_space=pl.ANY)
    dma = pltpu.SemaphoreType.DMA
    return pl.pallas_call(
        route_kernel,
        out_shape=(
            jax.ShapeDtypeStruct(slots, BF),
            jax.ShapeDtypeStruct((2, 2, RANK, D), BF),
        ),
        in_specs=[pl.BlockSpec(memory_space=pltpu.SMEM), anywhere, anywhere, anywhere],
        out_specs=(vmem, vmem),
        scratch_shapes=[
            pltpu.VMEM((MICRO, MB, D), BF),
            pltpu.VMEM(slots, BF),
            pltpu.VMEM(slots, BF),
            pltpu.VMEM((SPLIT, MB, D), BF),
            dma(()),
            dma((SPLIT,)),
            dma((SPLIT,)),
            dma((2 * FAR,)),
            dma((2 * FAR,)),
            dma((SPLIT,)),
            dma((2 * FAR,)),
            dma((2 * FAR,)),
            dma((2,)),
            dma((2,)),
        ],
        compiler_params=pltpu.CompilerParams(
            collective_id=0, has_side_effects=True, vmem_limit_bytes=32 << 20
        ),
        name="route",
    )(pick, inbox, w_in, w_out)


def split_peer(peer):
    return peer // 16, (peer // 2) % ROWS_Y, peer % 2


def join_peer(z, y, c):
    return z * 16 + y * 2 + c


HALF = 2 * RANK
SPREAD = [(dy, dz) for dy in (4, 3, 5, 2, 6, 1, 7, 0) for dz in (1, 0)]


def across(left, right):
    return lax.dot_general(left, right, (((1,), (1,)), ((), ())), preferred_element_type=F32)


def down(left, right):
    return lax.dot_general(left, right, (((0,), (0,)), ((), ())), preferred_element_type=F32)


def along(left, right):
    return jnp.dot(left, right, preferred_element_type=F32)


def mean_of(total):
    return jnp.sum(total, axis=-1, keepdims=True) / D


def section_kernel(
    source, taken, arrived, returned, weights, handed, total, hid, n0, n1, g1, l0, l1, b0, b1,
    terms, half, other_half, summed, landed, own, other, ss, rs, sc, rc
):
    section = lax.axis_index("section")
    z, y, c = split_peer(lax.axis_index("peer"))
    ahead = (section + 1) % SECTIONS
    behind = (section + SECTIONS - 1) % SECTIONS
    partner = (section, join_peer(z, y, 1 - c))
    mine = pl.ds(pl.multiple_of(c * HALF, HALF), HALF)
    theirs = pl.ds(pl.multiple_of((1 - c) * HALF, HALF), HALF)

    barrier = pltpu.get_barrier_semaphore()
    pl.semaphore_signal(barrier, inc=1, device_id=partner, device_id_type=MESH)
    for dy, dz in SPREAD:
        pl.semaphore_signal(
            barrier,
            inc=1,
            device_id=(ahead, join_peer((z + dz) % 2, (y + dy) % ROWS_Y, c)),
            device_id_type=MESH,
        )

    pieces = [pl.ds(k, CHUNK) for k in range(0, D, CHUNK)]

    def block(step, carry):
        rows = pl.ds(pl.multiple_of(step * BLOCK, BLOCK), BLOCK)
        square = jnp.zeros((BLOCK, 1), F32)
        for piece in pieces:
            parts = []
            for k in range(BLOCK // MB):
                slot = step * (BLOCK // MB) + k
                part = arrived[source[slot], :, piece].astype(F32)
                parts.append(part * taken[slot])
            x = jnp.concatenate(parts, axis=0)
            hid[:, piece] = x
            square += jnp.sum(x * x, axis=-1, keepdims=True)
        scale0 = lax.rsqrt(square / D + epsilon)
        low = jnp.zeros((BLOCK, RANK), F32)
        for piece in pieces:
            normed = (hid[:, piece] * scale0).astype(BF)
            n0[rows, piece] = normed
            low += across(normed, weights[0, 0, :, piece])
        low0 = low.astype(BF)
        l0[rows, :] = low0
        square = jnp.zeros((BLOCK, 1), F32)
        for piece in pieces:
            x = hid[:, piece] + along(low0, weights[1, 0, :, piece])
            hid[:, piece] = x
            square += jnp.sum(x * x, axis=-1, keepdims=True)
        scale1 = lax.rsqrt(square / D + epsilon)
        low = jnp.zeros((BLOCK, RANK), F32)
        back = jnp.zeros((BLOCK, RANK), F32)
        for piece in pieces:
            normed = (hid[:, piece] * scale1).astype(BF)
            n1[rows, piece] = normed
            low += across(normed, weights[0, 1, :, piece])
            back += across(returned[rows, piece], weights[1, 1, :, piece])
        low1 = low.astype(BF)
        back1 = back.astype(BF)
        l1[rows, :] = low1
        b1[rows, :] = back1
        both = jnp.zeros((BLOCK, 1), F32)
        for piece in pieces:
            x = hid[:, piece]
            handed[rows, piece] = (x + along(low1, weights[1, 1, :, piece])).astype(BF)
            spread = along(back1, weights[0, 1, :, piece])
            both += jnp.sum(spread * (x * scale1), axis=-1, keepdims=True)
        both = both / D
        back = jnp.zeros((BLOCK, RANK), F32)
        for piece in pieces:
            plain = hid[:, piece] * scale1
            spread = along(back1, weights[0, 1, :, piece])
            grad = returned[rows, piece].astype(F32) + scale1 * (spread - plain * both)
            grad = grad.astype(BF)
            g1[rows, piece] = grad
            back += across(grad, weights[1, 0, :, piece])
        b0[rows, :] = back.astype(BF)
        return carry

    lax.fori_loop(0, TOK // BLOCK, block, 0)
    def fill(dz, first, last):
        for k in range(first, last, CHUNK):
            piece = pl.ds(pl.multiple_of((z + dz) % 2 * (D // 2) + k, CHUNK), CHUNK)
            terms[0:16, piece] = down(b0[...], n0[:, piece])
            terms[16:32, piece] = down(b1[...], n1[:, piece])
            terms[32:48, piece] = down(l0[...], g1[:, piece])
            terms[48:64, piece] = down(l1[...], returned[:, piece])
            half[:, piece] = terms[theirs, piece].astype(BF)

    swaps = []
    for dz in (1, 0):
        columns = pl.ds(pl.multiple_of((z + dz) % 2 * (D // 2), D // 2), D // 2)
        swap = pltpu.make_async_remote_copy(
            src_ref=half.at[:, columns],
            dst_ref=other_half.at[:, columns],
            send_sem=sc.at[1 + dz],
            recv_sem=rc.at[1 + dz],
            device_id=partner,
            device_id_type=MESH,
        )
        swaps.append((dz, columns, swap))
    fill(1, 0, D // 2)
    pl.semaphore_wait(barrier, 1 + len(SPREAD))
    fill(0, 0, CHUNK)
    swaps[0][2].start()
    fill(0, CHUNK, D // 2)
    swaps[1][2].start()
    copies = []
    for dz, columns, swap in swaps:
        swap.wait_recv()
        summed[:, columns] = (terms[mine, columns] + other_half[:, columns].astype(F32)).astype(BF)
        for i, (dy, turn) in enumerate(SPREAD):
            if turn != dz:
                continue
            chip_z, chip_y = (z + dz) % 2, (y + dy) % ROWS_Y
            start = pl.multiple_of(128 * ((5 * (chip_z * ROWS_Y + chip_y)) // 2), 128)
            copy = pltpu.make_async_remote_copy(
                src_ref=summed.at[:, pl.ds(start, WINDOW)],
                dst_ref=landed.at[i],
                send_sem=ss.at[i],
                recv_sem=rs.at[i],
                device_id=(behind, join_peer(chip_z, chip_y, c)),
                device_id_type=MESH,
            )
            copy.start()
            copies.append(copy)
    for _, _, swap in swaps:
        swap.wait_send()
    for copy in copies:
        copy.wait()
    own[...] = jnp.sum(landed[...].astype(F32), axis=0)
    back = pltpu.make_async_remote_copy(
        src_ref=own,
        dst_ref=other,
        send_sem=sc.at[0],
        recv_sem=rc.at[0],
        device_id=partner,
        device_id_type=MESH,
    )
    back.start()
    back.wait()
    total[mine, :] = own[...] / PEERS
    total[theirs, :] = other[...] / PEERS


def section_step(source, taken, arrived, returned, weights):
    vmem = pl.BlockSpec(memory_space=pltpu.VMEM)
    smem = pl.BlockSpec(memory_space=pltpu.SMEM)
    return pl.pallas_call(
        section_kernel,
        out_shape=(
            jax.ShapeDtypeStruct((TOK, D), BF),
            jax.ShapeDtypeStruct((2 * HALF, WINDOW), F32),
        ),
        in_specs=[smem, smem, vmem, vmem, vmem],
        out_specs=(vmem, vmem),
        scratch_shapes=[
            pltpu.VMEM((BLOCK, D), F32),
            pltpu.VMEM((TOK, D), BF),
            pltpu.VMEM((TOK, D), BF),
            pltpu.VMEM((TOK, D), BF),
            pltpu.VMEM((TOK, RANK), BF),
            pltpu.VMEM((TOK, RANK), BF),
            pltpu.VMEM((TOK, RANK), BF),
            pltpu.VMEM((TOK, RANK), BF),
            pltpu.VMEM((2 * HALF, D), F32),
            pltpu.VMEM((HALF, D), BF),
            pltpu.VMEM((HALF, D), BF),
            pltpu.VMEM((HALF, D), BF),
            pltpu.VMEM((len(SPREAD), HALF, WINDOW), BF),
            pltpu.VMEM((HALF, WINDOW), F32),
            pltpu.VMEM((HALF, WINDOW), F32),
            pltpu.SemaphoreType.DMA((len(SPREAD),)),
            pltpu.SemaphoreType.DMA((len(SPREAD),)),
            pltpu.SemaphoreType.DMA((3,)),
            pltpu.SemaphoreType.DMA((3,)),
        ],
        compiler_params=pltpu.CompilerParams(
            collective_id=1, has_side_effects=True, vmem_limit_bytes=40 << 20
        ),
        name="section_step",
    )(source, taken, arrived, returned, weights)


def tables(routes, section, peer):
    row = lax.dynamic_index_in_dim(
        lax.dynamic_index_in_dim(routes, section, 0, keepdims=False), peer, 0, keepdims=False
    )
    behind = (section + SECTIONS - 1) % SECTIONS
    column = lax.dynamic_index_in_dim(
        lax.dynamic_index_in_dim(routes, behind, 0, keepdims=False), peer, 1, keepdims=False
    )
    index = jnp.arange(PEERS, dtype=jnp.int32)
    before = index[None, :] < index[:, None]
    pick = jnp.minimum(jnp.sum(jnp.where(before, row[None, :], 0), axis=1), MICRO - 1)
    slot = jnp.sum(jnp.where(before, column[None, :], 0), axis=1)
    x, y, z, c = place_of(section, peer)
    near_z = (z + 8 - jnp.where(x == 0, 1, 0)) % 8 // 4
    from_z, from_y, from_c = split_peer(index)
    turn = (y - from_y + ROWS_Y) % ROWS_Y
    order = jnp.asarray([dy for dy, dc in SLOTS if dc == 0], jnp.int32)
    place = jnp.sum(
        jnp.where(
            turn[:, None] == order[None, :], jnp.arange(ROWS_Y, dtype=jnp.int32)[None, :], 0
        ),
        axis=1,
    )
    step = place * 2 + jnp.where(from_z == near_z, FAR, 0) + jnp.where(from_c == c, 0, 1)
    here = (jnp.arange(CAP, dtype=jnp.int32)[:, None] == slot[None, :]) & (column[None, :] > 0)
    source = jnp.sum(jnp.where(here, step[None, :], 0), axis=1)
    taken = jnp.sum(here.astype(F32), axis=1)
    return pick, source, taken


def shards(inbox, routes, adapter_in, adapter_out, returned):
    section = lax.axis_index("section")
    peer = lax.axis_index("peer")
    pick, source, taken = tables(routes, section, peer)
    arrived, weights = route(
        pick, inbox.reshape(MICRO, MB, D), adapter_in[0], adapter_out[0]
    )
    handed, total = section_step(source, taken, arrived, returned[0, 0], weights)
    start = (peer // 2 % 2) * 64 + (peer % 2) * 160
    own = lax.dynamic_slice_in_dim(total, start, D // PEERS, axis=1).reshape(2, 2, RANK, D // PEERS)
    return handed[None, None], own[0][None], own[1][None]


def solution(mesh):
    return jax.shard_map(
        shards,
        mesh=mesh,
        in_specs=(
            P("section", "peer", None, None),
            P(),
            P("section", None, None, None),
            P("section", None, None, None),
            P("section", "peer", None, None),
        ),
        out_specs=(
            P("section", "peer", None, None),
            P("section", None, None, "peer"),
            P("section", None, None, "peer"),
        ),
        check_vma=False,
    )
```

```python
import jax
import jax.numpy as jnp
from jax import lax
from jax.experimental import pallas as pl
from jax.experimental.pallas import tpu as pltpu
from jax.sharding import PartitionSpec as P

MESH = pl.DeviceIdType.MESH
BF = jnp.bfloat16
F32 = jnp.float32

D = 5120
MB = 8
RANK = 16
SECTIONS = 16
PEERS = 32
ROWS_Y = 8
MICRO = 16
CAP = 20
TOK = CAP * MB
BLOCK = 160
CHUNK = 256
WINDOW = 384
epsilon = 1e-06

SLOTS = [(dy, dc) for dy in (4, 3, 5, 2, 6, 1, 7, 0) for dc in (0, 1)]
FAR = len(SLOTS)
SPLIT = 4
LAG = 4


def place_of(section, peer):
    z = (peer // 16) * 4 + section // 4
    return section % 4, (peer // 2) % ROWS_Y, z, peer % 2


def device_at(x, y, z, c):
    z = (z + 8) % 8
    return (z % 4) * 4 + (x + 4) % 4, (z // 4) * 16 + ((y + ROWS_Y) % ROWS_Y) * 2 + c


def route_kernel(
    pick, inbox, w_in, w_out, arrived, weights, mine, staged, relay, middle, load, s1, r1, s2, r2, s3, s4, r3, sw, rw
):
    x, y, z, c = place_of(lax.axis_index("section"), lax.axis_index("peer"))
    leaving, entering = x == 3, x == 0
    shift_out, shift_in = jnp.where(leaving, 1, 0), jnp.where(entering, 1, 0)
    in_plane = [(dy, dc) for dy in range(ROWS_Y) for dc in (0, 1) if dy or dc]

    fetch = pltpu.make_async_copy(inbox, mine, load)
    fetch.start()
    barrier = pltpu.get_barrier_semaphore()

    def greet(*where):
        pl.semaphore_signal(barrier, inc=1, device_id=device_at(*where), device_id_type=MESH)

    greet(x - 1, y, z - shift_in, c)
    greet(x - 1, y, z - shift_in - 4, c)

    @pl.when(entering)
    def _():
        greet(x - 1, y, z - 3, c)
        greet(x, y, z - 2, c)

    for dy, dc in in_plane:
        greet(x, y + dy, z, (c + dc) % 2)
    fetch.wait()
    for k, (dy, dc) in enumerate(SLOTS):
        for far in (1, 0):
            target = device_at(x + 1, y + dy, z + shift_out + 4 * far, (c + dc) % 2)[1]
            staged[k + FAR * (1 - far)] = mine[pick[target]]
    greeted = 2 + len(in_plane) + shift_out + shift_in
    pl.semaphore_wait(barrier, greeted)

    def send(source, target, send_sem, recv_sem, *where):
        return pltpu.make_async_remote_copy(
            src_ref=source,
            dst_ref=target,
            send_sem=send_sem,
            recv_sem=recv_sem,
            device_id=device_at(*where),
            device_id_type=MESH,
        )

    def weight_hop(source):
        return send(source, weights.at[c], sw.at[0], rw.at[0], x + 1, y, z + shift_out, c)

    near, far, outward, onward, final = [], [], [], [], []
    for k in range(FAR):
        far.append(
            send(
                staged.at[k], relay.at[k], s2.at[k], r2.at[k],
                x + 1, y, z + shift_out + 4, c,
            )
        )
        near.append(
            send(
                staged.at[FAR + k], relay.at[FAR + k], s2.at[FAR + k], r2.at[FAR + k],
                x + 1, y, z + shift_out, c,
            )
        )
    for k in range(SPLIT):
        outward.append(
            send(staged.at[k], middle.at[k], s1.at[k], r1.at[k], x + 1, y, z + 3, c)
        )
        onward.append(send(middle.at[k], relay.at[k], s3.at[k], r2.at[k], x, y, z + 2, c))
    for i in range(2 * FAR):
        dy, dc = SLOTS[i % FAR]
        if dy or dc:
            final.append(
                send(
                    relay.at[i], arrived.at[i], s4.at[i], r3.at[i],
                    x, y + dy, z, (c + dc) % 2,
                )
            )
        else:
            final.append(None)

    def pass_on(i):
        if final[i] is None:
            arrived[i] = relay[i]
        else:
            final[i].start()

    for k in range(FAR):
        if k < SPLIT:

            @pl.when(jnp.logical_not(leaving))
            def _():
                far[k].start()
        else:
            far[k].start()
        near[k].start()
        if 2 <= k < 2 + SPLIT:

            @pl.when(leaving)
            def _():
                outward[k - 2].start()

        if k == FAR - 3:

            @pl.when(c == 0)
            def _():
                weight_hop(w_in).start()

            @pl.when(c == 1)
            def _():
                weight_hop(w_out).start()

    share = send(weights.at[c], weights.at[c], sw.at[1], rw.at[1], x, y, z, 1 - c)
    order = list(range(SPLIT, FAR))
    order = order[:SPLIT] + list(range(SPLIT)) + order[SPLIT:]
    for t in range(FAR + LAG):
        if t < FAR:
            near[t].wait_recv()
            pass_on(FAR + t)
        if 2 <= t < 2 + SPLIT:

            @pl.when(entering)
            def _():
                outward[t - 2].wait_recv()
                onward[t - 2].start()
        if t == FAR:
            weight_hop(w_in).wait_recv()
            share.start()
        if t >= LAG:
            far[order[t - LAG]].wait_recv()
            pass_on(order[t - LAG])
    for k in range(FAR):
        near[k].wait_send()
        if k >= SPLIT:
            far[k].wait_send()

    @pl.when(leaving)
    def _():
        for copy in outward:
            copy.wait_send()

    @pl.when(jnp.logical_not(leaving))
    def _():
        for copy in far[:SPLIT]:
            copy.wait_send()

    @pl.when(entering)
    def _():
        for copy in onward:
            copy.wait_send()

    for copy in final:
        if copy is not None:
            copy.wait()
    weight_hop(w_in).wait_send()
    share.wait()


def route(pick, inbox, w_in, w_out):
    slots = (2 * FAR, MB, D)
    vmem = pl.BlockSpec(memory_space=pltpu.VMEM)
    anywhere = pl.BlockSpec(memory_space=pl.ANY)
    dma = pltpu.SemaphoreType.DMA
    return pl.pallas_call(
        route_kernel,
        out_shape=(
            jax.ShapeDtypeStruct(slots, BF),
            jax.ShapeDtypeStruct((2, 2, RANK, D), BF),
        ),
        in_specs=[pl.BlockSpec(memory_space=pltpu.SMEM), anywhere, anywhere, anywhere],
        out_specs=(vmem, vmem),
        scratch_shapes=[
            pltpu.VMEM((MICRO, MB, D), BF),
            pltpu.VMEM(slots, BF),
            pltpu.VMEM(slots, BF),
            pltpu.VMEM((SPLIT, MB, D), BF),
            dma(()),
            dma((SPLIT,)),
            dma((SPLIT,)),
            dma((2 * FAR,)),
            dma((2 * FAR,)),
            dma((SPLIT,)),
            dma((2 * FAR,)),
            dma((2 * FAR,)),
            dma((2,)),
            dma((2,)),
        ],
        compiler_params=pltpu.CompilerParams(
            collective_id=0, has_side_effects=True, vmem_limit_bytes=32 << 20
        ),
        name="route",
    )(pick, inbox, w_in, w_out)


def split_peer(peer):
    return peer // 16, (peer // 2) % ROWS_Y, peer % 2


def join_peer(z, y, c):
    return z * 16 + y * 2 + c


HALF = 2 * RANK
SPREAD = [(dy, dz) for dy in (4, 3, 5, 2, 6, 1, 7, 0) for dz in (1, 0)]


def across(left, right):
    return lax.dot_general(left, right, (((1,), (1,)), ((), ())), preferred_element_type=F32)


def down(left, right):
    return lax.dot_general(left, right, (((0,), (0,)), ((), ())), preferred_element_type=F32)


def along(left, right):
    return jnp.dot(left, right, preferred_element_type=F32)


def mean_of(total):
    return jnp.sum(total, axis=-1, keepdims=True) / D


def section_kernel(
    source, taken, arrived, returned, weights, handed, total, hid, n0, n1, g1, l0, l1, b0, b1,
    terms, half, other_half, summed, landed, own, other, ss, rs, sc, rc
):
    section = lax.axis_index("section")
    z, y, c = split_peer(lax.axis_index("peer"))
    ahead = (section + 1) % SECTIONS
    behind = (section + SECTIONS - 1) % SECTIONS
    partner = (section, join_peer(z, y, 1 - c))
    mine = pl.ds(pl.multiple_of(c * HALF, HALF), HALF)
    theirs = pl.ds(pl.multiple_of((1 - c) * HALF, HALF), HALF)

    barrier = pltpu.get_barrier_semaphore()
    pl.semaphore_signal(barrier, inc=1, device_id=partner, device_id_type=MESH)
    for dy, dz in SPREAD:
        pl.semaphore_signal(
            barrier,
            inc=1,
            device_id=(ahead, join_peer((z + dz) % 2, (y + dy) % ROWS_Y, c)),
            device_id_type=MESH,
        )

    pieces = [pl.ds(k, CHUNK) for k in range(0, D, CHUNK)]

    def block(step, carry):
        rows = pl.ds(pl.multiple_of(step * BLOCK, BLOCK), BLOCK)
        square = jnp.zeros((BLOCK, 1), F32)
        for piece in pieces:
            parts = []
            for k in range(BLOCK // MB):
                slot = step * (BLOCK // MB) + k
                part = arrived[source[slot], :, piece].astype(F32)
                parts.append(part * taken[slot])
            x = jnp.concatenate(parts, axis=0)
            hid[:, piece] = x
            square += jnp.sum(x * x, axis=-1, keepdims=True)
        scale0 = lax.rsqrt(square / D + epsilon)
        low = jnp.zeros((BLOCK, RANK), F32)
        for piece in pieces:
            normed = (hid[:, piece] * scale0).astype(BF)
            n0[rows, piece] = normed
            low += across(normed, weights[0, 0, :, piece])
        low0 = low.astype(BF)
        l0[rows, :] = low0
        square = jnp.zeros((BLOCK, 1), F32)
        for piece in pieces:
            x = hid[:, piece] + along(low0, weights[1, 0, :, piece])
            hid[:, piece] = x
            square += jnp.sum(x * x, axis=-1, keepdims=True)
        scale1 = lax.rsqrt(square / D + epsilon)
        low = jnp.zeros((BLOCK, RANK), F32)
        back = jnp.zeros((BLOCK, RANK), F32)
        for piece in pieces:
            normed = (hid[:, piece] * scale1).astype(BF)
            n1[rows, piece] = normed
            low += across(normed, weights[0, 1, :, piece])
            back += across(returned[rows, piece], weights[1, 1, :, piece])
        low1 = low.astype(BF)
        back1 = back.astype(BF)
        l1[rows, :] = low1
        b1[rows, :] = back1
        both = jnp.zeros((BLOCK, 1), F32)
        for piece in pieces:
            x = hid[:, piece]
            handed[rows, piece] = (x + along(low1, weights[1, 1, :, piece])).astype(BF)
            spread = along(back1, weights[0, 1, :, piece])
            both += jnp.sum(spread * (x * scale1), axis=-1, keepdims=True)
        both = both / D
        back = jnp.zeros((BLOCK, RANK), F32)
        for piece in pieces:
            plain = hid[:, piece] * scale1
            spread = along(back1, weights[0, 1, :, piece])
            grad = returned[rows, piece].astype(F32) + scale1 * (spread - plain * both)
            grad = grad.astype(BF)
            g1[rows, piece] = grad
            back += across(grad, weights[1, 0, :, piece])
        b0[rows, :] = back.astype(BF)
        return carry

    lax.fori_loop(0, TOK // BLOCK, block, 0)
    def fill(dz, first, last):
        for k in range(first, last, CHUNK):
            piece = pl.ds(pl.multiple_of((z + dz) % 2 * (D // 2) + k, CHUNK), CHUNK)
            terms[0:16, piece] = down(b0[...], n0[:, piece])
            terms[16:32, piece] = down(b1[...], n1[:, piece])
            terms[32:48, piece] = down(l0[...], g1[:, piece])
            terms[48:64, piece] = down(l1[...], returned[:, piece])
            half[:, piece] = terms[theirs, piece].astype(BF)

    swaps = []
    for dz in (1, 0):
        columns = pl.ds(pl.multiple_of((z + dz) % 2 * (D // 2), D // 2), D // 2)
        swap = pltpu.make_async_remote_copy(
            src_ref=half.at[:, columns],
            dst_ref=other_half.at[:, columns],
            send_sem=sc.at[1 + dz],
            recv_sem=rc.at[1 + dz],
            device_id=partner,
            device_id_type=MESH,
        )
        swaps.append((dz, columns, swap))
    fill(1, 0, D // 2)
    pl.semaphore_wait(barrier, 1 + len(SPREAD))
    fill(0, 0, CHUNK)
    swaps[0][2].start()
    fill(0, CHUNK, D // 2)
    swaps[1][2].start()
    copies = []
    for dz, columns, swap in swaps:
        swap.wait_recv()
        summed[:, columns] = (terms[mine, columns] + other_half[:, columns].astype(F32)).astype(BF)
        for i, (dy, turn) in enumerate(SPREAD):
            if turn != dz:
                continue
            chip_z, chip_y = (z + dz) % 2, (y + dy) % ROWS_Y
            start = pl.multiple_of(128 * ((5 * (chip_z * ROWS_Y + chip_y)) // 2), 128)
            copy = pltpu.make_async_remote_copy(
                src_ref=summed.at[:, pl.ds(start, WINDOW)],
                dst_ref=landed.at[i],
                send_sem=ss.at[i],
                recv_sem=rs.at[i],
                device_id=(behind, join_peer(chip_z, chip_y, c)),
                device_id_type=MESH,
            )
            copy.start()
            copies.append(copy)
    for _, _, swap in swaps:
        swap.wait_send()
    for copy in copies:
        copy.wait()
    own[...] = jnp.sum(landed[...].astype(F32), axis=0)
    back = pltpu.make_async_remote_copy(
        src_ref=own,
        dst_ref=other,
        send_sem=sc.at[0],
        recv_sem=rc.at[0],
        device_id=partner,
        device_id_type=MESH,
    )
    back.start()
    back.wait()
    total[mine, :] = own[...] / PEERS
    total[theirs, :] = other[...] / PEERS


def section_step(source, taken, arrived, returned, weights):
    vmem = pl.BlockSpec(memory_space=pltpu.VMEM)
    smem = pl.BlockSpec(memory_space=pltpu.SMEM)
    return pl.pallas_call(
        section_kernel,
        out_shape=(
            jax.ShapeDtypeStruct((TOK, D), BF),
            jax.ShapeDtypeStruct((2 * HALF, WINDOW), F32),
        ),
        in_specs=[smem, smem, vmem, vmem, vmem],
        out_specs=(vmem, vmem),
        scratch_shapes=[
            pltpu.VMEM((BLOCK, D), F32),
            pltpu.VMEM((TOK, D), BF),
            pltpu.VMEM((TOK, D), BF),
            pltpu.VMEM((TOK, D), BF),
            pltpu.VMEM((TOK, RANK), BF),
            pltpu.VMEM((TOK, RANK), BF),
            pltpu.VMEM((TOK, RANK), BF),
            pltpu.VMEM((TOK, RANK), BF),
            pltpu.VMEM((2 * HALF, D), F32),
            pltpu.VMEM((HALF, D), BF),
            pltpu.VMEM((HALF, D), BF),
            pltpu.VMEM((HALF, D), BF),
            pltpu.VMEM((len(SPREAD), HALF, WINDOW), BF),
            pltpu.VMEM((HALF, WINDOW), F32),
            pltpu.VMEM((HALF, WINDOW), F32),
            pltpu.SemaphoreType.DMA((len(SPREAD),)),
            pltpu.SemaphoreType.DMA((len(SPREAD),)),
            pltpu.SemaphoreType.DMA((3,)),
            pltpu.SemaphoreType.DMA((3,)),
        ],
        compiler_params=pltpu.CompilerParams(
            collective_id=1, has_side_effects=True, vmem_limit_bytes=40 << 20
        ),
        name="section_step",
    )(source, taken, arrived, returned, weights)


def tables(routes, section, peer):
    row = lax.dynamic_index_in_dim(
        lax.dynamic_index_in_dim(routes, section, 0, keepdims=False), peer, 0, keepdims=False
    )
    behind = (section + SECTIONS - 1) % SECTIONS
    column = lax.dynamic_index_in_dim(
        lax.dynamic_index_in_dim(routes, behind, 0, keepdims=False), peer, 1, keepdims=False
    )
    index = jnp.arange(PEERS, dtype=jnp.int32)
    before = index[None, :] < index[:, None]
    pick = jnp.minimum(jnp.sum(jnp.where(before, row[None, :], 0), axis=1), MICRO - 1)
    slot = jnp.sum(jnp.where(before, column[None, :], 0), axis=1)
    x, y, z, c = place_of(section, peer)
    near_z = (z + 8 - jnp.where(x == 0, 1, 0)) % 8 // 4
    from_z, from_y, from_c = split_peer(index)
    turn = (y - from_y + ROWS_Y) % ROWS_Y
    order = jnp.asarray([dy for dy, dc in SLOTS if dc == 0], jnp.int32)
    place = jnp.sum(
        jnp.where(
            turn[:, None] == order[None, :], jnp.arange(ROWS_Y, dtype=jnp.int32)[None, :], 0
        ),
        axis=1,
    )
    step = place * 2 + jnp.where(from_z == near_z, FAR, 0) + jnp.where(from_c == c, 0, 1)
    here = (jnp.arange(CAP, dtype=jnp.int32)[:, None] == slot[None, :]) & (column[None, :] > 0)
    source = jnp.sum(jnp.where(here, step[None, :], 0), axis=1)
    taken = jnp.sum(here.astype(F32), axis=1)
    return pick, source, taken


def shards(inbox, routes, adapter_in, adapter_out, returned):
    section = lax.axis_index("section")
    peer = lax.axis_index("peer")
    pick, source, taken = tables(routes, section, peer)
    arrived, weights = route(
        pick, inbox.reshape(MICRO, MB, D), adapter_in[0], adapter_out[0]
    )
    handed, total = section_step(source, taken, arrived, returned[0, 0], weights)
    start = (peer // 2 % 2) * 64 + (peer % 2) * 160
    own = lax.dynamic_slice_in_dim(total, start, D // PEERS, axis=1).reshape(2, 2, RANK, D // PEERS)
    return handed[None, None], own[0][None], own[1][None]


def solution(mesh):
    return jax.shard_map(
        shards,
        mesh=mesh,
        in_specs=(
            P("section", "peer", None, None),
            P(),
            P("section", None, None, None),
            P("section", None, None, None),
            P("section", "peer", None, None),
        ),
        out_specs=(
            P("section", "peer", None, None),
            P("section", None, None, "peer"),
            P("section", None, None, "peer"),
        ),
        check_vma=False,
    )
```
